32 devices in a mesh: dom: 8 (over z, core), rep: 4 (over y, x).
Axes of the slice: x: 2, y: 2, z: 4, core: 2. Of those that a mesh axis runs over, the one named last changes fastest.
Arguments:
- node_features: bfloat16 [16384, 256], P(('dom', 'rep')), may hold values from -6 to 6
- weight: bfloat16 [256, 256], replicated, may hold values from -0.375 to 0.375
- cotangent: bfloat16 [16384, 256], P(('dom', 'rep')), may hold values from -6 to 6
- tile_row: int32 [8, 4, 512], P('dom', 'rep'), may hold values from 0 to 15
- tile_col: int32 [8, 4, 512], P('dom', 'rep'), may hold values from 0 to 31
- tile_values: bfloat16 [8, 4, 512, 128, 128], P('dom', 'rep'), may hold values from -0.0625 to 0.0625
- tile_count: int32 [8, 4], P('dom', 'rep'), may hold values from 128 to 512, as said below
Outputs:
- output: bfloat16 [16384, 256], P(('dom', 'rep'))
- grad_features: bfloat16 [16384, 256], P(('dom', 'rep'))
- grad_weight: float32 [256, 256], replicated
The draws below stay inside these ranges and needn't reach their ends.
Inputs may be any that keep to these rules, and one draw needn't show every extreme that they name: Live slots are the first tile_count slots of each device's list; some device has all 512 slots live.
All inputs are finite; a program needn't handle non-finite values.
Results may differ from the reference program's by a relative error of at most 0.0061.
Values may be sent and summed in bfloat16 or wider, within the bound.
A program may use at most 192 MiB of HBM per device.

```python
import jax
import jax.numpy as jnp
from jax import lax

F = 256
S = 4
K = 512
NODES = 16384
N_DOM = 8
N_REP = 4


def draw_tile_count(key, part):
    counts = jax.random.randint(jax.random.fold_in(key, 11), (N_DOM * N_REP,), K // 4, K + 1)
    fullest = jax.random.randint(jax.random.fold_in(key, 12), (), 0, N_DOM * N_REP)
    counts = jnp.where(jnp.arange(N_DOM * N_REP) == fullest, K, counts)
    return counts.reshape(N_DOM, N_REP).astype(jnp.int32)


def place_ends(drawn, key, least, largest):
    longest = drawn.shape.index(max(drawn.shape))
    spots = []
    for shift in (0, 1):
        where = [jax.random.randint(jax.random.fold_in(key, axis), (), 0, length) for axis, length in enumerate(drawn.shape)]
        where[longest] = (where[longest] + shift) % drawn.shape[longest]
        spots.append(tuple(where))
    return drawn.at[spots[0]].set(least).at[spots[1]].set(largest)


def steps_of(stream_key, shape, pieces, least, largest):
    loudness, own = 1.0, jax.random.fold_in(stream_key, 6)
    for position, parts in pieces:
        steps = jnp.exp(jax.random.uniform(jax.random.fold_in(own, position), (parts,), jnp.float32, least / len(pieces), largest / len(pieces)))
        loudness = loudness * jnp.repeat(steps, shape[position] // parts).reshape([-1 if axis == position else 1 for axis in range(len(shape))])
    return loudness


def centred(key, shape, deviation, reach, split=(), held_as=jnp.bfloat16):
    gain = steps_of(key, shape, split, -0.22, 0.18) if split else 1.0
    result = jax.random.normal(key, shape, jnp.float32) * deviation * gain
    return jnp.minimum(jnp.maximum(result, -reach), reach).astype(held_as)


def setup_inputs(seed: int = 0) -> dict:
    streams_of = jax.random.split(jax.random.key(seed), 8)
    node_features = centred(streams_of[0], (NODES, F), 1.0, 6.0, ((0, 32),))
    weight = centred(streams_of[1], (F, F), F ** -0.5, 0.375)
    cotangent = centred(streams_of[2], (NODES, F), 1.0, 6.0, ((0, 32),))
    tile_row = place_ends(jax.random.randint(streams_of[3], (N_DOM, N_REP, K), 0, N_REP * S), jax.random.fold_in(streams_of[3], 1), 0, (N_REP * S) - 1).astype(jnp.int32)
    tile_col = place_ends(jax.random.randint(streams_of[4], (N_DOM, N_REP, K), 0, N_DOM * S), jax.random.fold_in(streams_of[4], 1), 0, (N_DOM * S) - 1).astype(jnp.int32)
    tile_values = centred(streams_of[5], (N_DOM, N_REP, K, 128, 128), (16 * K) ** -0.5, 0.0625, ((0, 8), (1, 4)))
    tile_count = draw_tile_count(jax.random.fold_in(streams_of[7], 71), 0)
    return dict(node_features=node_features, weight=weight, cotangent=cotangent, tile_row=tile_row, tile_col=tile_col, tile_values=tile_values, tile_count=tile_count)


def silu_slope(summed):
    sig = jax.nn.sigmoid(summed)
    return sig * (1.0 + summed * (1.0 - sig))


def spread(source, values, pick, place, active, flipped, total_blocks):
    pattern = "tba,tbf->taf" if flipped else "tab,tbf->taf"

    def one_device(accum, items):
        tiles, pick_index, place_index, enabled = items
        picked = source[pick_index].astype(jnp.float32)
        products = jnp.einsum(pattern, tiles.astype(jnp.float32), picked)
        products = products * enabled.astype(jnp.float32)[:, None, None]
        return accum.at[place_index].add(products), None

    start = jnp.zeros((total_blocks, 128, source.shape[2]), jnp.float32)
    accum, unused = lax.scan(one_device, start, (values, pick, place, active))
    return accum


def reference(node_features, weight, cotangent, tile_row, tile_col, tile_values, tile_count):
    blocks_part = N_REP * S
    total_blocks = NODES // 128
    projected = jnp.dot(node_features, weight, preferred_element_type=jnp.float32).astype(jnp.bfloat16)
    source = projected.reshape(total_blocks, 128, F)
    part_index = jnp.arange(N_DOM, dtype=jnp.int32)[:, None, None]
    repl_index = jnp.arange(N_REP, dtype=jnp.int32)[None, :, None]
    global_row = (part_index * blocks_part + tile_row).reshape(N_DOM * N_REP, K).astype(jnp.int32)
    global_col = ((tile_col // S) * blocks_part + repl_index * S + tile_col % S).reshape(N_DOM * N_REP, K).astype(jnp.int32)
    active = (jnp.arange(K, dtype=jnp.int32)[None, None, :] < tile_count[:, :, None]).reshape(N_DOM * N_REP, K)
    values = tile_values.reshape(N_DOM * N_REP, K, 128, 128)
    summed = spread(source, values, global_col, global_row, active, False, total_blocks).reshape(NODES, F)
    output = jax.nn.silu(summed).astype(jnp.bfloat16)
    grad_summed = (cotangent.astype(jnp.float32) * silu_slope(summed)).astype(jnp.bfloat16)
    back = spread(grad_summed.reshape(total_blocks, 128, F), values, global_row, global_col, active, True, total_blocks)
    grad_projected = back.reshape(NODES, F).astype(jnp.bfloat16)
    grad_features = jnp.dot(grad_projected, weight.T, preferred_element_type=jnp.float32).astype(jnp.bfloat16)
    grad_weight = jnp.dot(node_features.T, grad_projected, preferred_element_type=jnp.float32)
    return output, grad_features, grad_weight
```

```python
import functools

import jax
import jax.numpy as jnp
from jax import lax
from jax.experimental import pallas as pl
from jax.experimental.pallas import tpu as pltpu
from jax.sharding import PartitionSpec as P

CHUNKS = 8


def build_kernel(row_blocks, col_blocks, row_ref, col_ref, count_ref, tiles_ref, dense_ref, tiles, stage, head, after, in_sem, out_sem):
    slots = tiles.shape[0]
    per_chunk = slots // CHUNKS
    count = count_ref[0]
    loads = [
        pltpu.make_async_copy(
            tiles_ref.at[pl.ds(c * per_chunk, per_chunk)],
            tiles.at[pl.ds(c * per_chunk, per_chunk)],
            in_sem.at[c],
        )
        for c in range(CHUNKS)
    ]
    for c in range(CHUNKS):
        loads[c].start()

    def clear(p, carry):
        for u in range(8):
            head[p * 8 + u] = -1
        return carry

    lax.fori_loop(0, row_blocks * col_blocks // 8, clear, 0)

    def link(k, carry):
        place = row_ref[k] * col_blocks + col_ref[k]
        after[k] = head[place]
        head[place] = k
        return carry

    lax.fori_loop(0, count, link, 0)
    for c in range(CHUNKS):
        loads[c].wait()

    def out_copy(rb):
        slot = lax.rem(rb, 2)
        return pltpu.make_async_copy(
            stage.at[slot], dense_ref.at[pl.ds(pl.multiple_of(rb * 128, 128), 128)], out_sem.at[slot]
        )

    def one_row(rb, carry):
        slot = lax.rem(rb, 2)

        @pl.when(rb >= 2)
        def _():
            out_copy(rb - 2).wait()

        def one_place(cb, inner):
            first = head[rb * col_blocks + cb]
            start = jnp.maximum(first, 0)
            value = tiles[start].astype(jnp.float32)
            value = jnp.where(first >= 0, value, 0.0)
            follow = jnp.where(first >= 0, after[start], -1)

            def more(state):
                return state[0] >= 0

            def add(state):
                k, total = state
                return after[k], total + tiles[k].astype(jnp.float32)

            unused, value = lax.while_loop(more, add, (follow, value))
            stage[slot, :, pl.ds(pl.multiple_of(cb * 128, 128), 128)] = value.astype(jnp.bfloat16)
            return inner

        lax.fori_loop(0, col_blocks, one_place, 0)
        out_copy(rb).start()
        return carry

    lax.fori_loop(0, row_blocks, one_row, 0)
    out_copy(row_blocks - 2).wait()
    out_copy(row_blocks - 1).wait()


def build_dense(row_index, col_index, count, values, row_blocks, col_blocks):
    slots = values.shape[0]
    smem = pl.BlockSpec(memory_space=pltpu.SMEM)
    return pl.pallas_call(
        functools.partial(build_kernel, row_blocks, col_blocks),
        out_shape=jax.ShapeDtypeStruct((row_blocks * 128, col_blocks * 128), jnp.bfloat16),
        in_specs=[smem, smem, smem, pl.BlockSpec(memory_space=pl.ANY)],
        out_specs=pl.BlockSpec(memory_space=pl.ANY),
        scratch_shapes=[
            pltpu.VMEM((slots, 128, 128), jnp.bfloat16),
            pltpu.VMEM((2, 128, col_blocks * 128), jnp.bfloat16),
            pltpu.SMEM((row_blocks * col_blocks,), jnp.int32),
            pltpu.SMEM((slots,), jnp.int32),
            pltpu.SemaphoreType.DMA((CHUNKS,)),
            pltpu.SemaphoreType.DMA((2,)),
        ],
        name="build_dense",
        cost_estimate=pl.CostEstimate(
            flops=slots * 128 * 128, bytes_accessed=slots * 128 * 128 * 4, transcendentals=0
        ),
    )(row_index, col_index, count, values)


def body(node_features, weight, cotangent, tile_row, tile_col, tile_values, tile_count):
    rows_here, feature_width = node_features.shape
    dom_size = lax.axis_size("dom")
    rep_size = lax.axis_size("rep")
    slots = tile_row.shape[2]
    row_blocks = rep_size * rows_here // 128
    col_blocks = dom_size * rows_here // 128
    dense = build_dense(
        tile_row.reshape(slots),
        tile_col.reshape(slots),
        tile_count.reshape(1),
        tile_values.reshape(slots, 128, 128),
        row_blocks,
        col_blocks,
    )
    projected = jnp.dot(node_features, weight, preferred_element_type=jnp.float32).astype(jnp.bfloat16)
    source = lax.all_gather(projected, "dom", axis=0, tiled=True)
    partial = jnp.dot(dense, source, preferred_element_type=jnp.float32).astype(jnp.bfloat16)
    pieces = lax.all_to_all(
        partial.reshape(rep_size, rows_here, feature_width), "rep", 0, 0
    )
    summed = jnp.sum(pieces.astype(jnp.float32), axis=0)
    sig = jax.nn.sigmoid(summed)
    output = (summed * sig).astype(jnp.bfloat16)
    slope = sig * (1.0 + summed * (1.0 - sig))
    grad_own = (cotangent.astype(jnp.float32) * slope).astype(jnp.bfloat16)
    grad_block = lax.all_gather(grad_own, "rep", axis=0, tiled=True)
    back = lax.dot_general(
        dense, grad_block, (((0,), (0,)), ((), ())), preferred_element_type=jnp.float32
    ).astype(jnp.bfloat16)
    back_pieces = lax.all_to_all(
        back.reshape(dom_size, rows_here, feature_width), "dom", 0, 0
    )
    grad_projected = jnp.sum(back_pieces.astype(jnp.float32), axis=0).astype(jnp.bfloat16)
    grad_features = jnp.dot(grad_projected, weight.T, preferred_element_type=jnp.float32).astype(
        jnp.bfloat16
    )
    local_weight = jnp.dot(node_features.T, grad_projected, preferred_element_type=jnp.float32)
    grad_weight = lax.psum(local_weight, ("dom", "rep"))
    return (output, grad_features, grad_weight)


def solution(mesh):
    placed = (
        P(("dom", "rep"), None),
        P(),
        P(("dom", "rep"), None),
        P("dom", "rep", None),
        P("dom", "rep", None),
        P("dom", "rep", None, None, None),
        P("dom", "rep"),
    )
    return jax.shard_map(
        body,
        mesh=mesh,
        in_specs=placed,
        out_specs=(P(("dom", "rep"), None), P(("dom", "rep"), None), P()),
        check_vma=False,
    )
```

```python
import functools

import jax
import jax.numpy as jnp
from jax import lax
from jax.experimental import pallas as pl
from jax.experimental.pallas import tpu as pltpu
from jax.sharding import PartitionSpec as P

CHUNKS = 8


def build_kernel(row_blocks, col_blocks, row_ref, col_ref, count_ref, tiles_ref, dense_ref, tiles, stage, head, after, in_sem, out_sem):
    slots = tiles.shape[0]
    per_chunk = slots // CHUNKS
    count = count_ref[0]
    loads = [
        pltpu.make_async_copy(
            tiles_ref.at[pl.ds(c * per_chunk, per_chunk)],
            tiles.at[pl.ds(c * per_chunk, per_chunk)],
            in_sem.at[c],
        )
        for c in range(CHUNKS)
    ]
    for c in range(CHUNKS):
        loads[c].start()

    def clear(p, carry):
        for u in range(8):
            head[p * 8 + u] = -1
        return carry

    lax.fori_loop(0, row_blocks * col_blocks // 8, clear, 0)

    def link(k, carry):
        place = row_ref[k] * col_blocks + col_ref[k]
        after[k] = head[place]
        head[place] = k
        return carry

    lax.fori_loop(0, count, link, 0)
    for c in range(CHUNKS):
        loads[c].wait()

    def out_copy(rb):
        slot = lax.rem(rb, 2)
        return pltpu.make_async_copy(
            stage.at[slot], dense_ref.at[pl.ds(pl.multiple_of(rb * 128, 128), 128)], out_sem.at[slot]
        )

    def one_row(rb, carry):
        slot = lax.rem(rb, 2)

        @pl.when(rb >= 2)
        def _():
            out_copy(rb - 2).wait()

        def one_place(cb, inner):
            first = head[rb * col_blocks + cb]
            start = jnp.maximum(first, 0)
            value = tiles[start].astype(jnp.float32)
            value = jnp.where(first >= 0, value, 0.0)
            follow = jnp.where(first >= 0, after[start], -1)

            def more(state):
                return state[0] >= 0

            def add(state):
                k, total = state
                return after[k], total + tiles[k].astype(jnp.float32)

            unused, value = lax.while_loop(more, add, (follow, value))
            stage[slot, :, pl.ds(pl.multiple_of(cb * 128, 128), 128)] = value.astype(jnp.bfloat16)
            return inner

        lax.fori_loop(0, col_blocks, one_place, 0)
        out_copy(rb).start()
        return carry

    lax.fori_loop(0, row_blocks, one_row, 0)
    out_copy(row_blocks - 2).wait()
    out_copy(row_blocks - 1).wait()


def build_dense(row_index, col_index, count, values, row_blocks, col_blocks):
    slots = values.shape[0]
    smem = pl.BlockSpec(memory_space=pltpu.SMEM)
    return pl.pallas_call(
        functools.partial(build_kernel, row_blocks, col_blocks),
        out_shape=jax.ShapeDtypeStruct((row_blocks * 128, col_blocks * 128), jnp.bfloat16),
        in_specs=[smem, smem, smem, pl.BlockSpec(memory_space=pl.ANY)],
        out_specs=pl.BlockSpec(memory_space=pl.ANY),
        scratch_shapes=[
            pltpu.VMEM((slots, 128, 128), jnp.bfloat16),
            pltpu.VMEM((2, 128, col_blocks * 128), jnp.bfloat16),
            pltpu.SMEM((row_blocks * col_blocks,), jnp.int32),
            pltpu.SMEM((slots,), jnp.int32),
            pltpu.SemaphoreType.DMA((CHUNKS,)),
            pltpu.SemaphoreType.DMA((2,)),
        ],
        name="build_dense",
        cost_estimate=pl.CostEstimate(
            flops=slots * 128 * 128, bytes_accessed=slots * 128 * 128 * 4, transcendentals=0
        ),
    )(row_index, col_index, count, values)


MESH = pl.DeviceIdType.MESH


def layer_kernel(dom_size, rep_size, *refs):
    chips = dom_size // 2
    pieces = refs[:chips]
    (
        weight_ref, cot_ref, dense_ref, out_ref, gf_ref, gw_ref,
        source, tiles, part_send, part_recv, held, grads, back, pair, z_send, z_recv,
        gw1_send, gw1_recv, gw2_send, gw2_recv, gw3_recv,
        piece_sem, pair_src_send, pair_src_recv, tile_sem,
        part_ssem, part_rsem, grad_ssem, grad_rsem, pair_ssem, pair_rsem, z_ssem, z_rsem,
        gw1_ssem, gw1_rsem, gw2_ssem, gw2_rsem, gw3_ssem, gw3_rsem,
    ) = refs[chips:]
    rows, width = cot_ref.shape
    me_d, me_r = lax.axis_index("dom"), lax.axis_index("rep")
    chip, core = me_d // 2, lax.rem(me_d, 2)
    partner = chip * 2 + 1 - core
    share = width // dom_size

    def dom_peer(i):
        return lax.rem(me_d + i, dom_size)

    def rep_peer(i):
        return lax.rem(me_r + i, rep_size)

    def chip_at(i):
        return lax.rem(chip + i, chips)

    barrier = pltpu.get_barrier_semaphore()
    for i in range(1, dom_size):
        pl.semaphore_signal(barrier, inc=1, device_id=(dom_peer(i), me_r), device_id_type=MESH)
    for i in range(1, rep_size):
        pl.semaphore_signal(barrier, inc=1, device_id=(me_d, rep_peer(i)), device_id_type=MESH)

    def tile_load(t):
        ahead = rep_peer(t + 1)
        slot = lax.rem(t, 2)
        return pltpu.make_async_copy(
            dense_ref.at[pl.ds(pl.multiple_of(ahead * rows, rows), rows)], tiles.at[slot], tile_sem.at[slot]
        )

    tile_load(0).start()
    tile_load(1).start()
    locals_ = []
    for i in range(chips):
        spot = pl.ds(pl.multiple_of((chip_at(i) * 2 + core) * rows, rows), rows)
        locals_.append(pltpu.make_async_copy(pieces[i], source.at[spot], piece_sem.at[i]))
        locals_[-1].start()

    pl.semaphore_wait(barrier, dom_size + rep_size - 2)
    shared = []
    for i in range(chips):
        spot = pl.ds(pl.multiple_of((chip_at(i) * 2 + core) * rows, rows), rows)
        shared.append(
            pltpu.make_async_remote_copy(
                src_ref=pieces[i], dst_ref=source.at[spot],
                send_sem=pair_src_send.at[i], recv_sem=pair_src_recv.at[i],
                device_id=(partner, me_r), device_id_type=MESH,
            )
        )
        shared[-1].start()
    for i in range(chips):
        locals_[i].wait()
    for i in range(chips):
        shared[i].wait()

    def part_copy(t):
        return pltpu.make_async_remote_copy(
            src_ref=part_send.at[t], dst_ref=part_recv.at[t],
            send_sem=part_ssem.at[t], recv_sem=part_rsem.at[t],
            device_id=(me_d, rep_peer(t + 1)), device_id_type=MESH,
        )

    half = rows // 2

    def forward(t, carry):
        slot = lax.rem(t, 2)
        tile_load(t).wait()

        def one(h, inner):
            lines = pl.ds(pl.multiple_of(h * half, half), half)
            product = jnp.dot(tiles[slot, lines, :], source[...], preferred_element_type=jnp.float32)

            @pl.when(t < rep_size - 1)
            def _():
                part_send[t, lines, :] = product.astype(jnp.bfloat16)

            @pl.when(t == rep_size - 1)
            def _():
                held[lines, :] = product

            return inner

        lax.fori_loop(0, 2, one, 0)

        @pl.when(t < rep_size - 1)
        def _():
            part_copy(t).start()

        @pl.when(t + 2 < rep_size)
        def _():
            tile_load(t + 2).start()

        return carry

    lax.fori_loop(0, rep_size, forward, 0)
    for t in range(rep_size - 1):
        part_copy(t).wait_recv()

    weight = weight_ref[...]

    def finish(h, carry):
        lines = pl.ds(pl.multiple_of(h * 128, 128), 128)
        total = held[lines, :]
        for t in range(rep_size - 1):
            total = total + part_recv[t, lines, :].astype(jnp.float32)
        high = total.astype(jnp.bfloat16)
        low = (total - high.astype(jnp.float32)).astype(jnp.bfloat16)
        summed = jnp.dot(high, weight, preferred_element_type=jnp.float32) + jnp.dot(
            low, weight, preferred_element_type=jnp.float32
        )
        sig = jax.nn.sigmoid(summed)
        out_ref[lines, :] = (summed * sig).astype(jnp.bfloat16)
        slope = sig * (1.0 + summed * (1.0 - sig))
        grad = (cot_ref[lines, :].astype(jnp.float32) * slope).astype(jnp.bfloat16)
        grads[0, lines, :] = grad
        held[lines, :] = total
        return carry

    lax.fori_loop(0, rows // 128, finish, 0)

    def grad_copy(u):
        return pltpu.make_async_remote_copy(
            src_ref=grads.at[0], dst_ref=grads.at[u],
            send_sem=grad_ssem.at[u], recv_sem=grad_rsem.at[u],
            device_id=(me_d, rep_peer(u)), device_id_type=MESH,
        )

    for u in range(1, rep_size):
        grad_copy(u).start()

    total = held[...]
    high = total.astype(jnp.bfloat16)
    low = (total - high.astype(jnp.float32)).astype(jnp.bfloat16)
    own_grad = grads[0]
    over_rows = (((0,), (0,)), ((), ()))
    own_term = lax.dot_general(high, own_grad, over_rows, preferred_element_type=jnp.float32)
    own_term = own_term + lax.dot_general(low, own_grad, over_rows, preferred_element_type=jnp.float32)
    gw2_send[...] = own_term
    gw1_send[...] = own_term.astype(jnp.bfloat16).reshape(dom_size, share, width)

    def gw1_copy(i):
        return pltpu.make_async_remote_copy(
            src_ref=gw1_send.at[dom_peer(i)], dst_ref=gw1_recv.at[i],
            send_sem=gw1_ssem.at[i], recv_sem=gw1_rsem.at[i],
            device_id=(dom_peer(i), me_r), device_id_type=MESH,
        )

    for i in range(1, dom_size):
        gw1_copy(i).start()

    def gw2_copy(i):
        return pltpu.make_async_remote_copy(
            src_ref=gw2_recv.at[me_r], dst_ref=gw2_recv.at[me_r],
            send_sem=gw2_ssem.at[i], recv_sem=gw2_rsem.at[i],
            device_id=(me_d, rep_peer(i)), device_id_type=MESH,
        )

    def gw3_copy(i):
        return pltpu.make_async_remote_copy(
            src_ref=gw3_recv.at[me_d], dst_ref=gw3_recv.at[me_d],
            send_sem=gw3_ssem.at[i], recv_sem=gw3_rsem.at[i],
            device_id=(dom_peer(i), me_r), device_id_type=MESH,
        )

    def weight_second():
        for i in range(1, dom_size):
            gw1_copy(i).wait_recv()
        mine = gw2_send[pl.ds(pl.multiple_of(me_d * share, share), share), :]
        for i in range(1, dom_size):
            mine = mine + gw1_recv[i].astype(jnp.float32)
        gw2_recv[me_r] = mine
        for i in range(1, rep_size):
            gw2_copy(i).start()

    def weight_third():
        for i in range(1, rep_size):
            gw2_copy(i).wait_recv()
        mine = gw2_recv[0]
        for i in range(1, rep_size):
            mine = mine + gw2_recv[i]
        gw3_recv[me_d] = mine.astype(jnp.bfloat16)
        for i in range(1, dom_size):
            gw3_copy(i).start()

    def back_step(u, flipped, slot, d):
        lanes = pl.ds(pl.multiple_of(d * rows, rows), rows)
        product = jnp.dot(flipped, tiles[slot, :, lanes], preferred_element_type=jnp.float32)

        @pl.when(u == 0)
        def _():
            back[d] = product

        @pl.when(u > 0)
        def _():
            back[d] = back[d] + product

    def pair_copy(j):
        there = chip_at(j + 1)
        return pltpu.make_async_remote_copy(
            src_ref=back.at[there * 2 + 1 - core], dst_ref=pair.at[there],
            send_sem=pair_ssem.at[j], recv_sem=pair_rsem.at[j],
            device_id=(partner, me_r), device_id_type=MESH,
        )

    def z_copy(j):
        return pltpu.make_async_remote_copy(
            src_ref=z_send.at[j], dst_ref=z_recv.at[j],
            send_sem=z_ssem.at[j], recv_sem=z_rsem.at[j],
            device_id=(chip_at(j + 1) * 2 + core, me_r), device_id_type=MESH,
        )

    for u in range(rep_size):
        t = rep_size - 1 - u
        slot = t % 2
        if u > 0:
            grad_copy(u).wait_recv()
        if u >= 2:
            tile_load(t).wait()
        flipped = jnp.transpose(grads[u].astype(jnp.float32)).astype(jnp.bfloat16)
        if u < rep_size - 1:
            lax.fori_loop(0, dom_size, lambda d, c: (back_step(u, flipped, slot, d), c)[1], 0)
            if u + 2 < rep_size:
                tile_load(t - 2).start()
            if u == 1:
                weight_second()
            if u == 2:
                weight_third()
        else:

            def toward(j, carry):
                back_step(u, flipped, slot, chip_at(j + 1) * 2 + 1 - core)
                pair_copy(j).start()
                return carry

            def keep(j, carry):
                back_step(u, flipped, slot, chip_at(j + 1) * 2 + core)
                pair_copy(j).wait_recv()
                there = chip_at(j + 1)
                both = back[there * 2 + core] + pair[there]

                @pl.when(j < chips - 1)
                def _():
                    z_send[j] = both.astype(jnp.bfloat16)
                    z_copy(j).start()

                @pl.when(j == chips - 1)
                def _():
                    back[me_d] = both

                return carry

            lax.fori_loop(0, chips, toward, 0)
            lax.fori_loop(0, chips, keep, 0)

    for j in range(chips - 1):
        z_copy(j).wait_recv()
    total = back[me_d]
    for j in range(chips - 1):
        total = total + z_recv[j].astype(jnp.float32)
    grad_projected = jnp.transpose(total).astype(jnp.bfloat16)
    gf_ref[...] = lax.dot_general(
        grad_projected, weight_ref[...], (((1,), (1,)), ((), ())), preferred_element_type=jnp.float32
    ).astype(jnp.bfloat16)
    for i in range(1, dom_size):
        gw3_copy(i).wait_recv()
    gw_ref[...] = gw3_recv[...].astype(jnp.float32).reshape(width, width)
    for t in range(rep_size - 1):
        part_copy(t).wait_send()
    for u in range(1, rep_size):
        grad_copy(u).wait_send()
        gw2_copy(u).wait_send()
    for i in range(1, dom_size):
        gw1_copy(i).wait_send()
        gw3_copy(i).wait_send()
    for j in range(chips):
        pair_copy(j).wait_send()
    for j in range(chips - 1):
        z_copy(j).wait_send()


def run_layer(pieces, weight, cotangent, dense, dom_size, rep_size):
    rows, width = cotangent.shape
    chips = dom_size // 2
    share = width // dom_size
    here = pl.BlockSpec(memory_space=pltpu.VMEM)
    away = pl.BlockSpec(memory_space=pl.ANY)
    sems = lambda count: pltpu.SemaphoreType.DMA((count,))
    half, full = jnp.bfloat16, jnp.float32
    return pl.pallas_call(
        functools.partial(layer_kernel, dom_size, rep_size),
        out_shape=(
            jax.ShapeDtypeStruct((rows, width), half),
            jax.ShapeDtypeStruct((rows, width), half),
            jax.ShapeDtypeStruct((width, width), full),
        ),
        in_specs=[away] * chips + [here, here, away],
        out_specs=(here, here, here),
        scratch_shapes=[
            pltpu.VMEM((dom_size * rows, width), half),
            pltpu.VMEM((2, rows, dom_size * rows), half),
            pltpu.VMEM((rep_size - 1, rows, width), half),
            pltpu.VMEM((rep_size - 1, rows, width), half),
            pltpu.VMEM((rows, width), full),
            pltpu.VMEM((rep_size, rows, width), half),
            pltpu.VMEM((dom_size, width, rows), full),
            pltpu.VMEM((chips, width, rows), full),
            pltpu.VMEM((chips - 1, width, rows), half),
            pltpu.VMEM((chips - 1, width, rows), half),
            pltpu.VMEM((dom_size, share, width), half),
            pltpu.VMEM((dom_size, share, width), half),
            pltpu.VMEM((width, width), full),
            pltpu.VMEM((rep_size, share, width), full),
            pltpu.VMEM((dom_size, share, width), half),
            sems(chips), sems(chips), sems(chips), sems(2),
            sems(rep_size), sems(rep_size), sems(rep_size), sems(rep_size),
            sems(chips), sems(chips), sems(chips), sems(chips),
            sems(dom_size), sems(dom_size), sems(rep_size), sems(rep_size),
            sems(dom_size), sems(dom_size),
        ],
        name="layer",
        compiler_params=pltpu.CompilerParams(collective_id=0, has_side_effects=True),
    )(*pieces, weight, cotangent, dense)


def body(node_features, weight, cotangent, tile_row, tile_col, tile_values, tile_count):
    rows_here = node_features.shape[0]
    dom_size = lax.axis_size("dom")
    rep_size = lax.axis_size("rep")
    chips = dom_size // 2
    slots = tile_row.shape[2]
    pieces = [node_features]
    for step in range(1, chips):
        route = [(((chip + step) % chips) * 2 + core, chip * 2 + core) for chip in range(chips) for core in range(2)]
        pieces.append(lax.ppermute(node_features, "dom", route))
    dense = build_dense(
        tile_row.reshape(slots),
        tile_col.reshape(slots),
        tile_count.reshape(1),
        tile_values.reshape(slots, 128, 128),
        rep_size * rows_here // 128,
        dom_size * rows_here // 128,
    )
    return run_layer(pieces, weight, cotangent, dense, dom_size, rep_size)


def solution(mesh):
    placed = (
        P(("dom", "rep"), None),
        P(),
        P(("dom", "rep"), None),
        P("dom", "rep", None),
        P("dom", "rep", None),
        P("dom", "rep", None, None, None),
        P("dom", "rep"),
    )
    return jax.shard_map(
        body,
        mesh=mesh,
        in_specs=placed,
        out_specs=(P(("dom", "rep"), None), P(("dom", "rep"), None), P()),
        check_vma=False,
    )
```

```python
import functools

import jax
import jax.numpy as jnp
from jax import lax
from jax.experimental import pallas as pl
from jax.experimental.pallas import tpu as pltpu
from jax.sharding import PartitionSpec as P

CHUNKS = 8
SPLIT = 2


def build_kernel(row_blocks, col_blocks, row_ref, col_ref, count_ref, tiles_ref, dense_ref, tiles, stage, head, after, in_sem, out_sem):
    slots = tiles.shape[0]
    per_chunk = slots // CHUNKS
    count = count_ref[0]
    loads = [
        pltpu.make_async_copy(
            tiles_ref.at[pl.ds(c * per_chunk, per_chunk)],
            tiles.at[pl.ds(c * per_chunk, per_chunk)],
            in_sem.at[c],
        )
        for c in range(CHUNKS)
    ]
    for c in range(CHUNKS):
        loads[c].start()

    def clear(p, carry):
        for u in range(8):
            head[p * 8 + u] = -1
        return carry

    lax.fori_loop(0, row_blocks * col_blocks // 8, clear, 0)

    def link(k, carry):
        place = row_ref[k] * col_blocks + col_ref[k]
        after[k] = head[place]
        head[place] = k
        return carry

    lax.fori_loop(0, count, link, 0)
    for c in range(CHUNKS):
        loads[c].wait()

    def out_copy(rb):
        slot = lax.rem(rb, 2)
        return pltpu.make_async_copy(
            stage.at[slot], dense_ref.at[pl.ds(pl.multiple_of(rb * 128, 128), 128)], out_sem.at[slot]
        )

    def one_row(rb, carry):
        slot = lax.rem(rb, 2)

        @pl.when(rb >= 2)
        def _():
            out_copy(rb - 2).wait()

        def one_place(cb, inner):
            first = head[rb * col_blocks + cb]
            start = jnp.maximum(first, 0)
            value = tiles[start].astype(jnp.float32)
            value = jnp.where(first >= 0, value, 0.0)
            follow = jnp.where(first >= 0, after[start], -1)

            def more(state):
                return state[0] >= 0

            def add(state):
                k, total = state
                return after[k], total + tiles[k].astype(jnp.float32)

            unused, value = lax.while_loop(more, add, (follow, value))
            stage[slot, :, pl.ds(pl.multiple_of(cb * 128, 128), 128)] = value.astype(jnp.bfloat16)
            return inner

        lax.fori_loop(0, col_blocks, one_place, 0)
        out_copy(rb).start()
        return carry

    lax.fori_loop(0, row_blocks, one_row, 0)
    out_copy(row_blocks - 2).wait()
    out_copy(row_blocks - 1).wait()


def build_dense(row_index, col_index, count, values, row_blocks, col_blocks):
    slots = values.shape[0]
    smem = pl.BlockSpec(memory_space=pltpu.SMEM)
    return pl.pallas_call(
        functools.partial(build_kernel, row_blocks, col_blocks),
        out_shape=jax.ShapeDtypeStruct((row_blocks * 128, col_blocks * 128), jnp.bfloat16),
        in_specs=[smem, smem, smem, pl.BlockSpec(memory_space=pl.ANY)],
        out_specs=pl.BlockSpec(memory_space=pl.ANY),
        scratch_shapes=[
            pltpu.VMEM((slots, 128, 128), jnp.bfloat16),
            pltpu.VMEM((2, 128, col_blocks * 128), jnp.bfloat16),
            pltpu.SMEM((row_blocks * col_blocks,), jnp.int32),
            pltpu.SMEM((slots,), jnp.int32),
            pltpu.SemaphoreType.DMA((CHUNKS,)),
            pltpu.SemaphoreType.DMA((2,)),
        ],
        name="build_dense",
        compiler_params=pltpu.CompilerParams(
            vmem_limit_bytes=slots * 128 * 128 * 2 + 2 * 128 * col_blocks * 128 * 2 + 4 * 2**20
        ),
        cost_estimate=pl.CostEstimate(
            flops=slots * 128 * 128, bytes_accessed=slots * 128 * 128 * 4, transcendentals=0
        ),
    )(row_index, col_index, count, values)


MESH = pl.DeviceIdType.MESH


def layer_kernel(dom_size, rep_size, *refs):
    chips = dom_size // 2
    pieces = refs[:chips]
    (
        weight_ref, cot_ref, dense_ref, out_ref, gp_ref, gw_ref,
        source, tiles, part_send, part_recv, held, grads, back, pair, up_send, up_recv, down_send, down_recv,
        gw1_send, gw1_recv, gw2_send, gw2_recv, gw3_recv,
        piece_sem, pair_src_send, pair_src_recv, tile_sem,
        part_ssem, part_rsem, grad_ssem, grad_rsem, pair_ssem, pair_rsem, up_ssem, up_rsem, down_ssem, down_rsem,
        gw1_ssem, gw1_rsem, gw2_ssem, gw2_rsem, gw3_ssem, gw3_rsem,
    ) = refs[chips:]
    rows, width = cot_ref.shape
    me_d, me_r = lax.axis_index("dom"), lax.axis_index("rep")
    chip, core = me_d // 2, lax.rem(me_d, 2)
    partner = chip * 2 + 1 - core
    share = width // dom_size

    def dom_peer(i):
        return lax.rem(me_d + i, dom_size)

    def rep_peer(i):
        return lax.rem(me_r + i, rep_size)

    def chip_at(i):
        return lax.rem(chip + i, chips)

    barrier = pltpu.get_barrier_semaphore()
    for i in range(1, dom_size):
        pl.semaphore_signal(barrier, inc=1, device_id=(dom_peer(i), me_r), device_id_type=MESH)
    for i in range(1, rep_size):
        pl.semaphore_signal(barrier, inc=1, device_id=(me_d, rep_peer(i)), device_id_type=MESH)

    def tile_load(t):
        ahead = rep_peer(t + 1)
        slot = lax.rem(t, 2)
        return pltpu.make_async_copy(
            dense_ref.at[pl.ds(pl.multiple_of(ahead * rows, rows), rows)], tiles.at[slot], tile_sem.at[slot]
        )

    tile_load(0).start()
    tile_load(1).start()
    locals_ = []
    for i in range(chips):
        spot = pl.ds(pl.multiple_of((chip_at(i) * 2 + core) * rows, rows), rows)
        locals_.append(pltpu.make_async_copy(pieces[i], source.at[spot], piece_sem.at[i]))
        locals_[-1].start()

    pl.semaphore_wait(barrier, dom_size + rep_size - 2)
    shared = []
    for i in range(chips):
        spot = pl.ds(pl.multiple_of((chip_at(i) * 2 + core) * rows, rows), rows)
        shared.append(
            pltpu.make_async_remote_copy(
                src_ref=pieces[i], dst_ref=source.at[spot],
                send_sem=pair_src_send.at[i], recv_sem=pair_src_recv.at[i],
                device_id=(partner, me_r), device_id_type=MESH,
            )
        )
        shared[-1].start()
    for i in range(chips):
        locals_[i].wait()
    for i in range(chips):
        shared[i].wait()

    def part_copy(t):
        return pltpu.make_async_remote_copy(
            src_ref=part_send.at[t], dst_ref=part_recv.at[t],
            send_sem=part_ssem.at[t], recv_sem=part_rsem.at[t],
            device_id=(me_d, rep_peer(t + 1)), device_id_type=MESH,
        )

    half = rows // 2

    def forward(t, carry):
        slot = lax.rem(t, 2)
        tile_load(t).wait()

        def one(h, inner):
            lines = pl.ds(pl.multiple_of(h * half, half), half)
            product = jnp.dot(tiles[slot, lines, :], source[...], preferred_element_type=jnp.float32)

            @pl.when(t < rep_size - 1)
            def _():
                part_send[t, lines, :] = product.astype(jnp.bfloat16)

            @pl.when(t == rep_size - 1)
            def _():
                held[lines, :] = product

            return inner

        lax.fori_loop(0, 2, one, 0)

        @pl.when(t < rep_size - 1)
        def _():
            part_copy(t).start()

        @pl.when(t + 2 < rep_size)
        def _():
            tile_load(t + 2).start()

        return carry

    lax.fori_loop(0, rep_size, forward, 0)
    for t in range(rep_size - 1):
        part_copy(t).wait_recv()

    weight = weight_ref[...]

    def finish(h, carry):
        lines = pl.ds(pl.multiple_of(h * 128, 128), 128)
        total = held[lines, :]
        for t in range(rep_size - 1):
            total = total + part_recv[t, lines, :].astype(jnp.float32)
        high = total.astype(jnp.bfloat16)
        low = (total - high.astype(jnp.float32)).astype(jnp.bfloat16)
        summed = jnp.dot(high, weight, preferred_element_type=jnp.float32) + jnp.dot(
            low, weight, preferred_element_type=jnp.float32
        )
        sig = jax.nn.sigmoid(summed)
        out_ref[lines, :] = (summed * sig).astype(jnp.bfloat16)
        slope = sig * (1.0 + summed * (1.0 - sig))
        grad = (cot_ref[lines, :].astype(jnp.float32) * slope).astype(jnp.bfloat16)
        grads[0, lines, :] = grad
        held[lines, :] = total
        return carry

    lax.fori_loop(0, rows // 128, finish, 0)

    def grad_copy(u):
        return pltpu.make_async_remote_copy(
            src_ref=grads.at[0], dst_ref=grads.at[u],
            send_sem=grad_ssem.at[u], recv_sem=grad_rsem.at[u],
            device_id=(me_d, rep_peer(u)), device_id_type=MESH,
        )

    for u in range(1, rep_size):
        grad_copy(u).start()

    total = held[...]
    high = total.astype(jnp.bfloat16)
    low = (total - high.astype(jnp.float32)).astype(jnp.bfloat16)
    own_grad = grads[0]
    over_rows = (((0,), (0,)), ((), ()))
    own_term = lax.dot_general(high, own_grad, over_rows, preferred_element_type=jnp.float32)
    own_term = own_term + lax.dot_general(low, own_grad, over_rows, preferred_element_type=jnp.float32)
    gw2_send[...] = own_term
    gw1_send[...] = own_term.astype(jnp.bfloat16).reshape(dom_size, share, width)

    def gw1_copy(i):
        return pltpu.make_async_remote_copy(
            src_ref=gw1_send.at[dom_peer(i)], dst_ref=gw1_recv.at[i],
            send_sem=gw1_ssem.at[i], recv_sem=gw1_rsem.at[i],
            device_id=(dom_peer(i), me_r), device_id_type=MESH,
        )

    for i in range(1, dom_size):
        gw1_copy(i).start()

    def gw2_copy(i):
        return pltpu.make_async_remote_copy(
            src_ref=gw2_recv.at[me_r], dst_ref=gw2_recv.at[me_r],
            send_sem=gw2_ssem.at[i], recv_sem=gw2_rsem.at[i],
            device_id=(me_d, rep_peer(i)), device_id_type=MESH,
        )

    def gw3_copy(i):
        return pltpu.make_async_remote_copy(
            src_ref=gw3_recv.at[me_d], dst_ref=gw3_recv.at[me_d],
            send_sem=gw3_ssem.at[i], recv_sem=gw3_rsem.at[i],
            device_id=(dom_peer(i), me_r), device_id_type=MESH,
        )

    def weight_second():
        for i in range(1, dom_size):
            gw1_copy(i).wait_recv()
        mine = gw2_send[pl.ds(pl.multiple_of(me_d * share, share), share), :]
        for i in range(1, dom_size):
            mine = mine + gw1_recv[i].astype(jnp.float32)
        gw2_recv[me_r] = mine
        for i in range(1, rep_size):
            gw2_copy(i).start()

    def weight_third():
        for i in range(1, rep_size):
            gw2_copy(i).wait_recv()
        mine = gw2_recv[0]
        for i in range(1, rep_size):
            mine = mine + gw2_recv[i]
        gw3_recv[me_d] = mine.astype(jnp.bfloat16)
        for i in range(1, dom_size):
            gw3_copy(i).start()

    def back_step(u, flipped, slot, d):
        lanes = pl.ds(pl.multiple_of(d * rows, rows), rows)
        product = jnp.dot(flipped, tiles[slot, :, lanes], preferred_element_type=jnp.float32)

        @pl.when(u == 0)
        def _():
            back[d] = product

        @pl.when(u > 0)
        def _():
            back[d] = back[d] + product

    part = width // SPLIT

    def turn(j):
        odd = lax.rem(j, 2)
        return (1 - odd) * (chips - 1 - j // 2) + odd * (j // 2)

    def pair_copy(j):
        there = turn(j)
        return pltpu.make_async_remote_copy(
            src_ref=back.at[there * 2 + 1 - core], dst_ref=pair.at[there],
            send_sem=pair_ssem.at[j], recv_sem=pair_rsem.at[j],
            device_id=(partner, me_r), device_id_type=MESH,
        )

    def up_copy(q):
        return pltpu.make_async_remote_copy(
            src_ref=up_send.at[q], dst_ref=up_recv.at[q],
            send_sem=up_ssem.at[q], recv_sem=up_rsem.at[q],
            device_id=((chip + 1) * 2 + core, me_r), device_id_type=MESH,
        )

    def down_copy(q):
        return pltpu.make_async_remote_copy(
            src_ref=down_send.at[q], dst_ref=down_recv.at[q],
            send_sem=down_ssem.at[q], recv_sem=down_rsem.at[q],
            device_id=((chip - 1) * 2 + core, me_r), device_id_type=MESH,
        )

    def own_part(there, q):
        lines = pl.ds(pl.multiple_of(lax.rem(q, SPLIT) * part, part), part)
        return back[there * 2 + core, lines, :]

    def relay(tick):
        q_up = tick - chip
        q_down = tick - (chips - 1 - chip)

        @pl.when((chip > 0) & (q_up >= 0) & (q_up < SPLIT * (chips - 1 - chip)))
        def _():
            up_copy(q_up).wait_recv()
            up_send[q_up] = (
                own_part(chips - 1 - q_up // SPLIT, q_up) + up_recv[q_up].astype(jnp.float32)
            ).astype(jnp.bfloat16)
            up_copy(q_up).start()

        @pl.when((chip < chips - 1) & (q_down >= 0) & (q_down < SPLIT * chip))
        def _():
            down_copy(q_down).wait_recv()
            down_send[q_down] = (
                own_part(q_down // SPLIT, q_down) + down_recv[q_down].astype(jnp.float32)
            ).astype(jnp.bfloat16)
            down_copy(q_down).start()

    for u in range(rep_size):
        t = rep_size - 1 - u
        slot = t % 2
        if u > 0:
            grad_copy(u).wait_recv()
        if u >= 2:
            tile_load(t).wait()
        flipped = jnp.transpose(grads[u].astype(jnp.float32)).astype(jnp.bfloat16)
        if u < rep_size - 1:
            lax.fori_loop(0, dom_size, lambda d, c: (back_step(u, flipped, slot, d), c)[1], 0)
            if u + 2 < rep_size:
                tile_load(t - 2).start()
            if u == 1:
                weight_second()
            if u == 2:
                weight_third()
        else:

            def toward(j, carry):
                back_step(u, flipped, slot, turn(j) * 2 + 1 - core)
                pair_copy(j).start()
                return carry

            def keep(j, carry):
                there = turn(j)
                back_step(u, flipped, slot, there * 2 + core)
                pair_copy(j).wait_recv()
                back[there * 2 + core] = back[there * 2 + core] + pair[there]

                @pl.when((chip == 0) & (there > 0))
                def _():
                    for h in range(SPLIT):
                        q = (chips - 1 - there) * SPLIT + h
                        up_send[q] = own_part(there, q).astype(jnp.bfloat16)
                        up_copy(q).start()

                @pl.when((chip == chips - 1) & (there < chips - 1))
                def _():
                    for h in range(SPLIT):
                        q = there * SPLIT + h
                        down_send[q] = own_part(there, q).astype(jnp.bfloat16)
                        down_copy(q).start()

                return carry

            lax.fori_loop(0, chips, toward, 0)
            lax.fori_loop(0, chips, keep, 0)

    lax.fori_loop(1, SPLIT * (chips - 2) + 1, lambda tick, c: (relay(tick), c)[1], 0)

    for h in range(SPLIT):
        lines = pl.ds(h * part, part)

        @pl.when(chip > 0)
        def _():
            q = (chips - 1 - chip) * SPLIT + h
            up_copy(q).wait_recv()
            back[me_d, lines, :] = back[me_d, lines, :] + up_recv[q].astype(jnp.float32)

        @pl.when(chip < chips - 1)
        def _():
            q = chip * SPLIT + h
            down_copy(q).wait_recv()
            back[me_d, lines, :] = back[me_d, lines, :] + down_recv[q].astype(jnp.float32)

        gp_ref[lines, :] = back[me_d, lines, :].astype(jnp.bfloat16)

    for i in range(1, dom_size):
        gw3_copy(i).wait_recv()
    gw_ref[...] = gw3_recv[...].reshape(width, width)
    for t in range(rep_size - 1):
        part_copy(t).wait_send()
    for u in range(1, rep_size):
        grad_copy(u).wait_send()
        gw2_copy(u).wait_send()
    for i in range(1, dom_size):
        gw1_copy(i).wait_send()
        gw3_copy(i).wait_send()
    for j in range(chips):
        pair_copy(j).wait_send()

    def sent(q, carry):
        @pl.when((chip < chips - 1) & (q < SPLIT * (chips - 1 - chip)))
        def _():
            up_copy(q).wait_send()

        @pl.when((chip > 0) & (q < SPLIT * chip))
        def _():
            down_copy(q).wait_send()

        return carry

    lax.fori_loop(0, SPLIT * (chips - 1), sent, 0)


def finish_kernel(raw_ref, gp_ref, gw_in_ref, weight_ref, out_ref, gf_ref, gw_ref):
    out_ref[...] = raw_ref[...]
    gw_ref[...] = gw_in_ref[...].astype(jnp.float32)
    grad_projected = jnp.transpose(gp_ref[...])
    gf_ref[...] = lax.dot_general(
        grad_projected, weight_ref[...], (((1,), (1,)), ((), ())), preferred_element_type=jnp.float32
    ).astype(jnp.bfloat16)


def finish(raw, grad_projected, grad_weight, weight):
    here = pl.BlockSpec(memory_space=pltpu.VMEM)
    return pl.pallas_call(
        finish_kernel,
        out_shape=(
            jax.ShapeDtypeStruct(raw.shape, jnp.bfloat16),
            jax.ShapeDtypeStruct(raw.shape, jnp.bfloat16),
            jax.ShapeDtypeStruct(grad_weight.shape, jnp.float32),
        ),
        in_specs=[here] * 4,
        out_specs=(here, here, here),
        name="finish",
        compiler_params=pltpu.CompilerParams(vmem_limit_bytes=16 * 2**20),
    )(raw, grad_projected, grad_weight, weight)


def room(scratch, extra):
    total = 0
    for item in scratch:
        if getattr(item, "memory_space", None) == pltpu.VMEM:
            size = jnp.dtype(item.dtype).itemsize
            for length in item.shape:
                size *= length
            total += size
    return total + extra


def run_layer(pieces, weight, cotangent, dense, dom_size, rep_size):
    rows, width = cotangent.shape
    chips = dom_size // 2
    share = width // dom_size
    here = pl.BlockSpec(memory_space=pltpu.VMEM)
    away = pl.BlockSpec(memory_space=pl.ANY)
    sems = lambda count: pltpu.SemaphoreType.DMA((count,))
    half, full = jnp.bfloat16, jnp.float32
    hops = SPLIT * (chips - 1)
    scratch = [
        pltpu.VMEM((dom_size * rows, width), half),
        pltpu.VMEM((2, rows, dom_size * rows), half),
        pltpu.VMEM((rep_size - 1, rows, width), half),
        pltpu.VMEM((rep_size - 1, rows, width), half),
        pltpu.VMEM((rows, width), full),
        pltpu.VMEM((rep_size, rows, width), half),
        pltpu.VMEM((dom_size, width, rows), full),
        pltpu.VMEM((chips, width, rows), full),
        pltpu.VMEM((hops, width // SPLIT, rows), half),
        pltpu.VMEM((hops, width // SPLIT, rows), half),
        pltpu.VMEM((hops, width // SPLIT, rows), half),
        pltpu.VMEM((hops, width // SPLIT, rows), half),
        pltpu.VMEM((dom_size, share, width), half),
        pltpu.VMEM((dom_size, share, width), half),
        pltpu.VMEM((width, width), full),
        pltpu.VMEM((rep_size, share, width), full),
        pltpu.VMEM((dom_size, share, width), half),
        sems(chips), sems(chips), sems(chips), sems(2),
        sems(rep_size), sems(rep_size), sems(rep_size), sems(rep_size),
        sems(chips), sems(chips), sems(hops), sems(hops), sems(hops), sems(hops),
        sems(dom_size), sems(dom_size), sems(rep_size), sems(rep_size),
        sems(dom_size), sems(dom_size),
    ]
    return pl.pallas_call(
        functools.partial(layer_kernel, dom_size, rep_size),
        out_shape=(
            jax.ShapeDtypeStruct((rows, width), half),
            jax.ShapeDtypeStruct((width, rows), half),
            jax.ShapeDtypeStruct((width, width), half),
        ),
        in_specs=[away] * chips + [here, here, away],
        out_specs=(here, here, here),
        scratch_shapes=scratch,
        name="layer",
        compiler_params=pltpu.CompilerParams(
            collective_id=0, has_side_effects=True, vmem_limit_bytes=room(scratch, 8 * 2**20)
        ),
    )(*pieces, weight, cotangent, dense)


def body(node_features, weight, cotangent, tile_row, tile_col, tile_values, tile_count):
    rows_here = node_features.shape[0]
    dom_size = lax.axis_size("dom")
    rep_size = lax.axis_size("rep")
    chips = dom_size // 2
    slots = tile_row.shape[2]
    pieces = [node_features]
    for step in range(1, chips):
        route = [(((chip + step) % chips) * 2 + core, chip * 2 + core) for chip in range(chips) for core in range(2)]
        pieces.append(lax.ppermute(node_features, "dom", route))
    dense = build_dense(
        tile_row.reshape(slots),
        tile_col.reshape(slots),
        tile_count.reshape(1),
        tile_values.reshape(slots, 128, 128),
        rep_size * rows_here // 128,
        dom_size * rows_here // 128,
    )
    raw, grad_projected, grad_weight = run_layer(pieces, weight, cotangent, dense, dom_size, rep_size)
    return tuple(finish(raw, grad_projected, grad_weight, weight))


def solution(mesh):
    placed = (
        P(("dom", "rep"), None),
        P(),
        P(("dom", "rep"), None),
        P("dom", "rep", None),
        P("dom", "rep", None),
        P("dom", "rep", None, None, None),
        P("dom", "rep"),
    )
    return jax.shard_map(
        body,
        mesh=mesh,
        in_specs=placed,
        out_specs=(P(("dom", "rep"), None), P(("dom", "rep"), None), P()),
        check_vma=False,
    )
```

```python
import functools

import jax
import jax.numpy as jnp
from jax import lax
from jax.experimental import pallas as pl
from jax.experimental.pallas import tpu as pltpu
from jax.sharding import PartitionSpec as P

CHUNKS = 8
SPLIT = 4


def build_kernel(row_blocks, col_blocks, row_ref, col_ref, count_ref, tiles_ref, dense_ref, tiles, stage, head, after, in_sem, out_sem):
    slots = tiles.shape[0]
    per_chunk = slots // CHUNKS
    count = count_ref[0]
    loads = [
        pltpu.make_async_copy(
            tiles_ref.at[pl.ds(c * per_chunk, per_chunk)],
            tiles.at[pl.ds(c * per_chunk, per_chunk)],
            in_sem.at[c],
        )
        for c in range(CHUNKS)
    ]
    for c in range(CHUNKS):
        loads[c].start()

    def clear(p, carry):
        for u in range(8):
            head[p * 8 + u] = -1
        return carry

    lax.fori_loop(0, row_blocks * col_blocks // 8, clear, 0)

    def link(k, carry):
        place = row_ref[k] * col_blocks + col_ref[k]
        after[k] = head[place]
        head[place] = k
        return carry

    lax.fori_loop(0, count, link, 0)
    for c in range(CHUNKS):
        loads[c].wait()

    def out_copy(rb):
        slot = lax.rem(rb, 2)
        return pltpu.make_async_copy(
            stage.at[slot], dense_ref.at[pl.ds(pl.multiple_of(rb * 128, 128), 128)], out_sem.at[slot]
        )

    def one_row(rb, carry):
        slot = lax.rem(rb, 2)

        @pl.when(rb >= 2)
        def _():
            out_copy(rb - 2).wait()

        def one_place(cb, inner):
            first = head[rb * col_blocks + cb]
            start = jnp.maximum(first, 0)
            value = tiles[start].astype(jnp.float32)
            value = jnp.where(first >= 0, value, 0.0)
            follow = jnp.where(first >= 0, after[start], -1)

            def more(state):
                return state[0] >= 0

            def add(state):
                k, total = state
                return after[k], total + tiles[k].astype(jnp.float32)

            unused, value = lax.while_loop(more, add, (follow, value))
            stage[slot, :, pl.ds(pl.multiple_of(cb * 128, 128), 128)] = value.astype(jnp.bfloat16)
            return inner

        lax.fori_loop(0, col_blocks, one_place, 0)
        out_copy(rb).start()
        return carry

    lax.fori_loop(0, row_blocks, one_row, 0)
    out_copy(row_blocks - 2).wait()
    out_copy(row_blocks - 1).wait()


def build_dense(row_index, col_index, count, values, row_blocks, col_blocks):
    slots = values.shape[0]
    smem = pl.BlockSpec(memory_space=pltpu.SMEM)
    return pl.pallas_call(
        functools.partial(build_kernel, row_blocks, col_blocks),
        out_shape=jax.ShapeDtypeStruct((row_blocks * 128, col_blocks * 128), jnp.bfloat16),
        in_specs=[smem, smem, smem, pl.BlockSpec(memory_space=pl.ANY)],
        out_specs=pl.BlockSpec(memory_space=pl.ANY),
        scratch_shapes=[
            pltpu.VMEM((slots, 128, 128), jnp.bfloat16),
            pltpu.VMEM((2, 128, col_blocks * 128), jnp.bfloat16),
            pltpu.SMEM((row_blocks * col_blocks,), jnp.int32),
            pltpu.SMEM((slots,), jnp.int32),
            pltpu.SemaphoreType.DMA((CHUNKS,)),
            pltpu.SemaphoreType.DMA((2,)),
        ],
        name="build_dense",
        compiler_params=pltpu.CompilerParams(
            vmem_limit_bytes=slots * 128 * 128 * 2 + 2 * 128 * col_blocks * 128 * 2 + 4 * 2**20
        ),
        cost_estimate=pl.CostEstimate(
            flops=slots * 128 * 128, bytes_accessed=slots * 128 * 128 * 4, transcendentals=0
        ),
    )(row_index, col_index, count, values)


MESH = pl.DeviceIdType.MESH


def layer_kernel(dom_size, rep_size, *refs):
    chips = dom_size // 2
    pieces = refs[:chips]
    (
        weight_ref, cot_ref, dense_ref, out_ref, gp_ref, gw_ref,
        source, tiles, part_send, part_recv, held, grads, back, pair, up_send, up_recv, down_send, down_recv,
        gw1_send, gw1_recv, gw2_send, gw2_recv, gw3_recv,
        piece_sem, pair_src_send, pair_src_recv, tile_sem,
        part_ssem, part_rsem, grad_ssem, grad_rsem, pair_ssem, pair_rsem, up_ssem, up_rsem, down_ssem, down_rsem,
        gw1_ssem, gw1_rsem, gw2_ssem, gw2_rsem, gw3_ssem, gw3_rsem,
    ) = refs[chips:]
    rows, width = cot_ref.shape
    me_d, me_r = lax.axis_index("dom"), lax.axis_index("rep")
    chip, core = me_d // 2, lax.rem(me_d, 2)
    partner = chip * 2 + 1 - core
    share = width // dom_size

    def dom_peer(i):
        return lax.rem(me_d + i, dom_size)

    def rep_peer(i):
        return lax.rem(me_r + i, rep_size)

    def chip_at(i):
        return lax.rem(chip + i, chips)

    barrier = pltpu.get_barrier_semaphore()
    for i in range(1, dom_size):
        pl.semaphore_signal(barrier, inc=1, device_id=(dom_peer(i), me_r), device_id_type=MESH)
    for i in range(1, rep_size):
        pl.semaphore_signal(barrier, inc=1, device_id=(me_d, rep_peer(i)), device_id_type=MESH)

    def tile_load(t):
        ahead = rep_peer(t + 1)
        slot = lax.rem(t, 2)
        return pltpu.make_async_copy(
            dense_ref.at[pl.ds(pl.multiple_of(ahead * rows, rows), rows)], tiles.at[slot], tile_sem.at[slot]
        )

    tile_load(0).start()
    tile_load(1).start()
    locals_ = []
    for i in range(chips):
        spot = pl.ds(pl.multiple_of((chip_at(i) * 2 + core) * rows, rows), rows)
        locals_.append(pltpu.make_async_copy(pieces[i], source.at[spot], piece_sem.at[i]))
        locals_[-1].start()

    pl.semaphore_wait(barrier, dom_size + rep_size - 2)
    shared = []
    for i in range(chips):
        spot = pl.ds(pl.multiple_of((chip_at(i) * 2 + core) * rows, rows), rows)
        shared.append(
            pltpu.make_async_remote_copy(
                src_ref=pieces[i], dst_ref=source.at[spot],
                send_sem=pair_src_send.at[i], recv_sem=pair_src_recv.at[i],
                device_id=(partner, me_r), device_id_type=MESH,
            )
        )
        shared[-1].start()
    for i in range(chips):
        locals_[i].wait()
    for i in range(chips):
        shared[i].wait()

    def part_copy(t):
        return pltpu.make_async_remote_copy(
            src_ref=part_send.at[t], dst_ref=part_recv.at[t],
            send_sem=part_ssem.at[t], recv_sem=part_rsem.at[t],
            device_id=(me_d, rep_peer(t + 1)), device_id_type=MESH,
        )

    half = rows // 2

    def forward(t, carry):
        slot = lax.rem(t, 2)
        tile_load(t).wait()

        def one(h, inner):
            lines = pl.ds(pl.multiple_of(h * half, half), half)
            product = jnp.dot(tiles[slot, lines, :], source[...], preferred_element_type=jnp.float32)

            @pl.when(t < rep_size - 1)
            def _():
                part_send[t, lines, :] = product.astype(jnp.bfloat16)

            @pl.when(t == rep_size - 1)
            def _():
                held[lines, :] = product

            return inner

        lax.fori_loop(0, 2, one, 0)

        @pl.when(t < rep_size - 1)
        def _():
            part_copy(t).start()

        @pl.when(t + 2 < rep_size)
        def _():
            tile_load(t + 2).start()

        return carry

    lax.fori_loop(0, rep_size, forward, 0)
    for t in range(rep_size - 1):
        part_copy(t).wait_recv()

    weight = weight_ref[...]

    def finish(h, carry):
        lines = pl.ds(pl.multiple_of(h * 128, 128), 128)
        total = held[lines, :]
        for t in range(rep_size - 1):
            total = total + part_recv[t, lines, :].astype(jnp.float32)
        high = total.astype(jnp.bfloat16)
        low = (total - high.astype(jnp.float32)).astype(jnp.bfloat16)
        summed = jnp.dot(high, weight, preferred_element_type=jnp.float32) + jnp.dot(
            low, weight, preferred_element_type=jnp.float32
        )
        sig = jax.nn.sigmoid(summed)
        out_ref[lines, :] = (summed * sig).astype(jnp.bfloat16)
        slope = sig * (1.0 + summed * (1.0 - sig))
        grad = (cot_ref[lines, :].astype(jnp.float32) * slope).astype(jnp.bfloat16)
        grads[0, lines, :] = grad
        held[lines, :] = total
        return carry

    lax.fori_loop(0, rows // 128, finish, 0)

    def grad_copy(u):
        return pltpu.make_async_remote_copy(
            src_ref=grads.at[0], dst_ref=grads.at[u],
            send_sem=grad_ssem.at[u], recv_sem=grad_rsem.at[u],
            device_id=(me_d, rep_peer(u)), device_id_type=MESH,
        )

    for u in range(1, rep_size):
        grad_copy(u).start()

    total = held[...]
    high = total.astype(jnp.bfloat16)
    low = (total - high.astype(jnp.float32)).astype(jnp.bfloat16)
    own_grad = grads[0]
    over_rows = (((0,), (0,)), ((), ()))
    own_term = lax.dot_general(high, own_grad, over_rows, preferred_element_type=jnp.float32)
    own_term = own_term + lax.dot_general(low, own_grad, over_rows, preferred_element_type=jnp.float32)
    gw2_send[...] = own_term
    gw1_send[...] = own_term.astype(jnp.bfloat16).reshape(dom_size, share, width)

    def gw1_copy(i):
        return pltpu.make_async_remote_copy(
            src_ref=gw1_send.at[dom_peer(i)], dst_ref=gw1_recv.at[i],
            send_sem=gw1_ssem.at[i], recv_sem=gw1_rsem.at[i],
            device_id=(dom_peer(i), me_r), device_id_type=MESH,
        )

    for i in range(1, dom_size):
        gw1_copy(i).start()

    def gw2_copy(i):
        return pltpu.make_async_remote_copy(
            src_ref=gw2_recv.at[me_r], dst_ref=gw2_recv.at[me_r],
            send_sem=gw2_ssem.at[i], recv_sem=gw2_rsem.at[i],
            device_id=(me_d, rep_peer(i)), device_id_type=MESH,
        )

    def gw3_copy(i):
        return pltpu.make_async_remote_copy(
            src_ref=gw3_recv.at[me_d], dst_ref=gw3_recv.at[me_d],
            send_sem=gw3_ssem.at[i], recv_sem=gw3_rsem.at[i],
            device_id=(dom_peer(i), me_r), device_id_type=MESH,
        )

    def weight_second():
        for i in range(1, dom_size):
            gw1_copy(i).wait_recv()
        mine = gw2_send[pl.ds(pl.multiple_of(me_d * share, share), share), :]
        for i in range(1, dom_size):
            mine = mine + gw1_recv[i].astype(jnp.float32)
        gw2_recv[me_r] = mine
        for i in range(1, rep_size):
            gw2_copy(i).start()

    def weight_third():
        for i in range(1, rep_size):
            gw2_copy(i).wait_recv()
        mine = gw2_recv[0]
        for i in range(1, rep_size):
            mine = mine + gw2_recv[i]
        gw3_recv[me_d] = mine.astype(jnp.bfloat16)
        for i in range(1, dom_size):
            gw3_copy(i).start()

    def back_step(u, flipped, slot, d):
        lanes = pl.ds(pl.multiple_of(d * rows, rows), rows)
        product = jnp.dot(flipped, tiles[slot, :, lanes], preferred_element_type=jnp.float32)

        @pl.when(u == 0)
        def _():
            back[d] = product

        @pl.when(u > 0)
        def _():
            back[d] = back[d] + product

    part = width // SPLIT

    def turn(j):
        odd = lax.rem(j, 2)
        return (1 - odd) * (chips - 1 - j // 2) + odd * (j // 2)

    def pair_copy(j):
        there = turn(j)
        return pltpu.make_async_remote_copy(
            src_ref=back.at[there * 2 + 1 - core], dst_ref=pair.at[there],
            send_sem=pair_ssem.at[j], recv_sem=pair_rsem.at[j],
            device_id=(partner, me_r), device_id_type=MESH,
        )

    def up_copy(q):
        return pltpu.make_async_remote_copy(
            src_ref=up_send.at[q], dst_ref=up_recv.at[q],
            send_sem=up_ssem.at[q], recv_sem=up_rsem.at[q],
            device_id=((chip + 1) * 2 + core, me_r), device_id_type=MESH,
        )

    def down_copy(q):
        return pltpu.make_async_remote_copy(
            src_ref=down_send.at[q], dst_ref=down_recv.at[q],
            send_sem=down_ssem.at[q], recv_sem=down_rsem.at[q],
            device_id=((chip - 1) * 2 + core, me_r), device_id_type=MESH,
        )

    def own_part(there, q):
        lines = pl.ds(pl.multiple_of(lax.rem(q, SPLIT) * part, part), part)
        return back[there * 2 + core, lines, :]

    def relay(tick):
        q_up = tick - chip
        q_down = tick - (chips - 1 - chip)

        @pl.when((chip > 0) & (q_up >= 0) & (q_up < SPLIT * (chips - 1 - chip)))
        def _():
            up_copy(q_up).wait_recv()
            up_send[q_up] = (
                own_part(chips - 1 - q_up // SPLIT, q_up) + up_recv[q_up].astype(jnp.float32)
            ).astype(jnp.bfloat16)
            up_copy(q_up).start()

        @pl.when((chip < chips - 1) & (q_down >= 0) & (q_down < SPLIT * chip))
        def _():
            down_copy(q_down).wait_recv()
            down_send[q_down] = (
                own_part(q_down // SPLIT, q_down) + down_recv[q_down].astype(jnp.float32)
            ).astype(jnp.bfloat16)
            down_copy(q_down).start()

    for u in range(rep_size):
        t = rep_size - 1 - u
        slot = t % 2
        if u > 0:
            grad_copy(u).wait_recv()
        if u >= 2:
            tile_load(t).wait()
        flipped = jnp.transpose(grads[u].astype(jnp.float32)).astype(jnp.bfloat16)
        if u < rep_size - 1:
            lax.fori_loop(0, dom_size, lambda d, c: (back_step(u, flipped, slot, d), c)[1], 0)
            if u + 2 < rep_size:
                tile_load(t - 2).start()
            if u == 1:
                weight_second()
            if u == 2:
                weight_third()
        else:

            def toward(j, carry):
                back_step(u, flipped, slot, turn(j) * 2 + 1 - core)
                pair_copy(j).start()
                return carry

            def keep(j, carry):
                there = turn(j)
                back_step(u, flipped, slot, there * 2 + core)
                pair_copy(j).wait_recv()
                back[there * 2 + core] = back[there * 2 + core] + pair[there]

                @pl.when((chip == 0) & (there > 0))
                def _():
                    for h in range(SPLIT):
                        q = (chips - 1 - there) * SPLIT + h
                        up_send[q] = own_part(there, q).astype(jnp.bfloat16)
                        up_copy(q).start()

                @pl.when((chip == chips - 1) & (there < chips - 1))
                def _():
                    for h in range(SPLIT):
                        q = there * SPLIT + h
                        down_send[q] = own_part(there, q).astype(jnp.bfloat16)
                        down_copy(q).start()

                return carry

            lax.fori_loop(0, chips, toward, 0)
            lax.fori_loop(0, chips, keep, 0)

    lax.fori_loop(1, SPLIT * (chips - 2) + 1, lambda tick, c: (relay(tick), c)[1], 0)

    for h in range(SPLIT):
        lines = pl.ds(h * part, part)

        @pl.when(chip > 0)
        def _():
            q = (chips - 1 - chip) * SPLIT + h
            up_copy(q).wait_recv()
            back[me_d, lines, :] = back[me_d, lines, :] + up_recv[q].astype(jnp.float32)

        @pl.when(chip < chips - 1)
        def _():
            q = chip * SPLIT + h
            down_copy(q).wait_recv()
            back[me_d, lines, :] = back[me_d, lines, :] + down_recv[q].astype(jnp.float32)

        gp_ref[lines, :] = back[me_d, lines, :].astype(jnp.bfloat16)

    for i in range(1, dom_size):
        gw3_copy(i).wait_recv()
    gw_ref[...] = gw3_recv[...].reshape(width, width)
    for t in range(rep_size - 1):
        part_copy(t).wait_send()
    for u in range(1, rep_size):
        grad_copy(u).wait_send()
        gw2_copy(u).wait_send()
    for i in range(1, dom_size):
        gw1_copy(i).wait_send()
        gw3_copy(i).wait_send()
    for j in range(chips):
        pair_copy(j).wait_send()

    def sent(q, carry):
        @pl.when((chip < chips - 1) & (q < SPLIT * (chips - 1 - chip)))
        def _():
            up_copy(q).wait_send()

        @pl.when((chip > 0) & (q < SPLIT * chip))
        def _():
            down_copy(q).wait_send()

        return carry

    lax.fori_loop(0, SPLIT * (chips - 1), sent, 0)


def finish_kernel(raw_ref, gp_ref, gw_in_ref, weight_ref, out_ref, gf_ref, gw_ref):
    out_ref[...] = raw_ref[...]
    gw_ref[...] = gw_in_ref[...].astype(jnp.float32)
    grad_projected = jnp.transpose(gp_ref[...])
    gf_ref[...] = lax.dot_general(
        grad_projected, weight_ref[...], (((1,), (1,)), ((), ())), preferred_element_type=jnp.float32
    ).astype(jnp.bfloat16)


def finish(raw, grad_projected, grad_weight, weight):
    here = pl.BlockSpec(memory_space=pltpu.VMEM)
    return pl.pallas_call(
        finish_kernel,
        out_shape=(
            jax.ShapeDtypeStruct(raw.shape, jnp.bfloat16),
            jax.ShapeDtypeStruct(raw.shape, jnp.bfloat16),
            jax.ShapeDtypeStruct(grad_weight.shape, jnp.float32),
        ),
        in_specs=[here] * 4,
        out_specs=(here, here, here),
        name="finish",
        compiler_params=pltpu.CompilerParams(vmem_limit_bytes=16 * 2**20),
    )(raw, grad_projected, grad_weight, weight)


def room(scratch, extra):
    total = 0
    for item in scratch:
        if getattr(item, "memory_space", None) == pltpu.VMEM:
            size = jnp.dtype(item.dtype).itemsize
            for length in item.shape:
                size *= length
            total += size
    return total + extra


def run_layer(pieces, weight, cotangent, dense, dom_size, rep_size):
    rows, width = cotangent.shape
    chips = dom_size // 2
    share = width // dom_size
    here = pl.BlockSpec(memory_space=pltpu.VMEM)
    away = pl.BlockSpec(memory_space=pl.ANY)
    sems = lambda count: pltpu.SemaphoreType.DMA((count,))
    half, full = jnp.bfloat16, jnp.float32
    hops = SPLIT * (chips - 1)
    scratch = [
        pltpu.VMEM((dom_size * rows, width), half),
        pltpu.VMEM((2, rows, dom_size * rows), half),
        pltpu.VMEM((rep_size - 1, rows, width), half),
        pltpu.VMEM((rep_size - 1, rows, width), half),
        pltpu.VMEM((rows, width), full),
        pltpu.VMEM((rep_size, rows, width), half),
        pltpu.VMEM((dom_size, width, rows), full),
        pltpu.VMEM((chips, width, rows), full),
        pltpu.VMEM((hops, width // SPLIT, rows), half),
        pltpu.VMEM((hops, width // SPLIT, rows), half),
        pltpu.VMEM((hops, width // SPLIT, rows), half),
        pltpu.VMEM((hops, width // SPLIT, rows), half),
        pltpu.VMEM((dom_size, share, width), half),
        pltpu.VMEM((dom_size, share, width), half),
        pltpu.VMEM((width, width), full),
        pltpu.VMEM((rep_size, share, width), full),
        pltpu.VMEM((dom_size, share, width), half),
        sems(chips), sems(chips), sems(chips), sems(2),
        sems(rep_size), sems(rep_size), sems(rep_size), sems(rep_size),
        sems(chips), sems(chips), sems(hops), sems(hops), sems(hops), sems(hops),
        sems(dom_size), sems(dom_size), sems(rep_size), sems(rep_size),
        sems(dom_size), sems(dom_size),
    ]
    return pl.pallas_call(
        functools.partial(layer_kernel, dom_size, rep_size),
        out_shape=(
            jax.ShapeDtypeStruct((rows, width), half),
            jax.ShapeDtypeStruct((width, rows), half),
            jax.ShapeDtypeStruct((width, width), half),
        ),
        in_specs=[away] * chips + [here, here, away],
        out_specs=(here, here, here),
        scratch_shapes=scratch,
        name="layer",
        compiler_params=pltpu.CompilerParams(
            collective_id=0, has_side_effects=True, vmem_limit_bytes=room(scratch, 8 * 2**20)
        ),
    )(*pieces, weight, cotangent, dense)


def body(node_features, weight, cotangent, tile_row, tile_col, tile_values, tile_count):
    rows_here = node_features.shape[0]
    dom_size = lax.axis_size("dom")
    rep_size = lax.axis_size("rep")
    chips = dom_size // 2
    slots = tile_row.shape[2]
    pieces = [node_features]
    for step in range(1, chips):
        route = [(((chip + step) % chips) * 2 + core, chip * 2 + core) for chip in range(chips) for core in range(2)]
        pieces.append(lax.ppermute(node_features, "dom", route))
    dense = build_dense(
        tile_row.reshape(slots),
        tile_col.reshape(slots),
        tile_count.reshape(1),
        tile_values.reshape(slots, 128, 128),
        rep_size * rows_here // 128,
        dom_size * rows_here // 128,
    )
    raw, grad_projected, grad_weight = run_layer(pieces, weight, cotangent, dense, dom_size, rep_size)
    return tuple(finish(raw, grad_projected, grad_weight, weight))


def solution(mesh):
    placed = (
        P(("dom", "rep"), None),
        P(),
        P(("dom", "rep"), None),
        P("dom", "rep", None),
        P("dom", "rep", None),
        P("dom", "rep", None, None, None),
        P("dom", "rep"),
    )
    return jax.shard_map(
        body,
        mesh=mesh,
        in_specs=placed,
        out_specs=(P(("dom", "rep"), None), P(("dom", "rep"), None), P()),
        check_vma=False,
    )
```
